32 devices in a mesh: dp: 8 (over y, x, core), tensor: 4 (over z).
Axes of the slice: x: 2, y: 2, z: 4, core: 2. Of those that a mesh axis runs over, the one named last changes fastest.
Arguments:
- block_input: float32 [8192, 1024], P(('dp', 'tensor')), may hold values from -40 to 40
- norm_gains: bfloat16 [2, 1024], P(None, 'dp'), may hold values from 0.5 to 1.5
- w_qkv: bfloat16 [3, 1024, 1024], P(None, 'dp', 'tensor'), may hold values from -2 to 2
- w_out: bfloat16 [1024, 1024], P('dp', 'tensor'), may hold values from -1.5 to 1.5
- w_in: bfloat16 [2, 1024, 2624], P(None, 'dp', 'tensor'), may hold values from -0.1875 to 0.1875
- w_down: bfloat16 [1024, 2624], P('dp', 'tensor'), may hold values from -0.125 to 0.125
- segment_ids: int32 [8, 1024], P('dp'), may hold values from 0 to 3, as said below
- cotangent: float32 [8192, 1024], P(('dp', 'tensor')), may hold values from -6 to 6
Outputs:
- block_output: float32 [8192, 1024], P(('dp', 'tensor'))
- grad_input: float32 [8192, 1024], P(('dp', 'tensor'))
- grad_qkv: float32 [3, 1024, 1024], P(None, 'dp', 'tensor')
- grad_out: float32 [1024, 1024], P('dp', 'tensor')
- grad_in: float32 [2, 1024, 2624], P(None, 'dp', 'tensor')
- grad_down: float32 [1024, 2624], P('dp', 'tensor')
- grad_gains: float32 [2, 1024], P(None, 'dp')
The draws below stay inside these ranges and needn't reach their ends.
Inputs may be any that keep to these rules, and one draw needn't show every extreme that they name: `segment_ids`: each row never falls and starts at 0; every sequence holds all 4 documents, each of 128 tokens or more, and in some sequence the last document holds exactly 128.
All inputs are finite; a program needn't handle non-finite values.
Results may differ from the reference program's by a relative error of at most 0.02.
Values may be sent and summed in bfloat16 or wider, within the bound.
A program may use at most 128 MiB of HBM per device.

```python
import jax
import jax.numpy as jnp
from jax import lax

D = 1024
HEADS = 16
HEAD_DIM = 64
FF = 2624
SEQ_LEN = 1024
DOCS = 4
SEQS = 8
TOKENS = 8192


def doc_starts(key):
    key_cuts, key_pick = jax.random.split(key, 2)
    base_len = SEQ_LEN // 8
    spare = SEQ_LEN - DOCS * base_len
    cuts = jax.random.randint(key_cuts, (SEQS, DOCS - 1), 0, spare + 1).astype(jnp.int32)
    chosen = jax.random.randint(key_pick, (), 0, SEQS).astype(jnp.int32)
    rows_here = jnp.arange(SEQS, dtype=jnp.int32)[:, None] == chosen
    last_cut = jnp.arange(DOCS - 1, dtype=jnp.int32)[None, :] == DOCS - 2
    cuts = jnp.where(rows_here & last_cut, spare, cuts).astype(jnp.int32)
    cuts = jnp.sort(cuts, axis=1)
    edges = jnp.concatenate([jnp.zeros((SEQS, 1), jnp.int32), cuts], axis=1)
    return (edges + base_len * jnp.arange(DOCS, dtype=jnp.int32)[None, :]).astype(jnp.int32)


def draw_segment_ids(key, part):
    starts = doc_starts(jax.random.fold_in(key, 11))
    places = jnp.arange(SEQ_LEN, dtype=jnp.int32)
    passed = (places[None, :, None] >= starts[:, None, 1:]).astype(jnp.int32)
    return jnp.sum(passed, axis=-1).astype(jnp.int32)


def draw_block_input(key, part):
    key_one = jax.random.fold_in(key, 0)
    result = jax.random.normal(key_one, (TOKENS, D), jnp.float32)
    return jnp.clip(result, -40.0, 40.0).astype(jnp.float32)


def draw_w_qkv(key, part):
    key_one = jax.random.fold_in(key, 0)
    base_w = jax.random.normal(key_one, (3, D, HEADS * HEAD_DIM), jnp.float32) * D ** (-0.5)
    return jnp.clip(base_w, -2.0, 2.0).astype(jnp.bfloat16)


def shard_levels(own_key, shape, shards, low, high):
    gain, own = 1.0, jax.random.fold_in(own_key, 6)
    for position, blocks in shards:
        heights = jnp.exp(jax.random.uniform(jax.random.fold_in(own, position), (blocks,), jnp.float32, low / len(shards), high / len(shards)))
        gain = gain * jnp.repeat(heights, shape[position] // blocks).reshape([-1 if axis == position else 1 for axis in range(len(shape))])
    return gain


def bell_draw(own_key, extent, scale, limit, cuts=(), kind=jnp.bfloat16):
    entries = jax.random.normal(own_key, extent, jnp.float32) * scale
    if len(cuts) > 0:
        entries = shard_levels(own_key, extent, cuts, -0.22, 0.18) * entries
    return jnp.clip(entries, min=-limit, max=limit).astype(kind)


def setup_inputs(seed: int = 0) -> dict:
    seeds = jax.random.split(jax.random.key(seed), 9)
    block_input = draw_block_input(jax.random.fold_in(seeds[8], 71), 0)
    norm_gains = jnp.clip(1.0 + 0.1 * jax.random.normal(seeds[1], (2, D), jnp.float32), 0.5, 1.5).astype(jnp.bfloat16)
    w_qkv = draw_w_qkv(jax.random.fold_in(seeds[8], 71), 0)
    w_out = bell_draw(seeds[3], (D, HEADS * HEAD_DIM), (HEADS * HEAD_DIM // 64) ** -0.5, 1.5, ((0, 8), (1, 4)))
    w_in = bell_draw(seeds[4], (2, D, FF), D ** -0.5, 0.1875, ((1, 8), (2, 4)))
    w_down = bell_draw(seeds[5], (D, FF), FF ** -0.5, 0.125, ((0, 8), (1, 4)))
    segment_ids = draw_segment_ids(jax.random.fold_in(seeds[8], 71), 0)
    cotangent = bell_draw(seeds[7], (TOKENS, D), 1.0, 6.0, ((0, 32),), jnp.float32)
    return {"block_input": block_input, "norm_gains": norm_gains, "w_qkv": w_qkv, "w_out": w_out, "w_in": w_in, "w_down": w_down, "segment_ids": segment_ids, "cotangent": cotangent}


EPS = 1e-05
ROPE_BASE = 160000.0
NEG_FILL = -1e+30

def layer_norm(rows_in):
    row_mean = lax.optimization_barrier(jnp.mean(rows_in, axis=-1, keepdims=True))
    centred = rows_in - row_mean
    inv_std = lax.rsqrt(lax.optimization_barrier(jnp.mean(centred * centred, axis=-1, keepdims=True)) + EPS)
    return (centred * inv_std, inv_std)

def norm_back(d_normed, normal_rows, inv_std, gain_row):
    scaled = d_normed * gain_row
    first_mean = lax.optimization_barrier(jnp.mean(scaled, axis=-1, keepdims=True))
    second_mean = lax.optimization_barrier(jnp.mean(scaled * normal_rows, axis=-1, keepdims=True))
    return inv_std * (scaled - first_mean - normal_rows * second_mean)

def rotary_tables(positions):
    half_dim = HEAD_DIM // 2
    freqs = ROPE_BASE ** (-2.0 * jnp.arange(half_dim).astype(jnp.float32) / HEAD_DIM)
    angles = positions.astype(jnp.float32)[:, None] * freqs[None, :]
    return (jnp.cos(angles), jnp.sin(angles))

def rotate(field, cosine, sine_tab):
    half_dim = field.shape[-1] // 2
    first_half = field[..., :half_dim]
    second_half = field[..., half_dim:]
    cos_b = cosine[:, None, :]
    sin_b = sine_tab[:, None, :]
    return jnp.concatenate([first_half * cos_b - second_half * sin_b, second_half * cos_b + first_half * sin_b], axis=-1)

def gelu_parts(gate_pre):
    normal_cdf = 0.5 * (1.0 + lax.erf(gate_pre * 0.7071067811865476))
    normal_pdf = jnp.exp(-0.5 * gate_pre * gate_pre) * 0.3989422804014327
    return (normal_cdf, normal_pdf)

def positions_of(seg_ids):
    seq_len = seg_ids.shape[1]
    which = (seg_ids[:, :, None] == jnp.arange(DOCS, dtype=jnp.int32)[None, None, :]).astype(jnp.int32)
    counts = lax.optimization_barrier(jnp.sum(which, axis=1)).astype(jnp.int32)
    doc_first = (jnp.cumsum(counts, axis=1) - counts).astype(jnp.int32)
    starts = lax.optimization_barrier(jnp.sum(which * doc_first[:, None, :], axis=-1)).astype(jnp.int32)
    return (jnp.arange(seq_len, dtype=jnp.int32)[None, :] - starts).astype(jnp.int32)

def reference(block_input, norm_gains, w_qkv, w_out, w_in, w_down, segment_ids, cotangent):
    gains = norm_gains.astype(jnp.float32)
    score_scale = HEAD_DIM ** (-0.5)
    qkv_wide = w_qkv.astype(jnp.float32)
    positions = positions_of(segment_ids)
    width = HEADS * HEAD_DIM

    def one_sequence(running, packed):
        rows_in, cot_rows, seg_row, pos_row = packed
        normal_one, inv_one = layer_norm(rows_in)
        normed_one = (normal_one * gains[0]).astype(jnp.bfloat16)
        projected = jnp.einsum('td,jde->jte', normed_one.astype(jnp.float32), qkv_wide)
        cosine, sine_tab = rotary_tables(pos_row)
        shaped = projected.reshape(3, SEQ_LEN, HEADS, HEAD_DIM)
        queries = rotate(shaped[0], cosine, sine_tab).astype(jnp.bfloat16)
        key_rows = rotate(shaped[1], cosine, sine_tab).astype(jnp.bfloat16)
        values = shaped[2].astype(jnp.bfloat16)
        same_doc = seg_row[:, None] == seg_row[None, :]
        scores = jnp.einsum('qhd,khd->hqk', queries.astype(jnp.float32), key_rows.astype(jnp.float32)) * score_scale
        scores = jnp.where(same_doc[None], scores, NEG_FILL)
        row_top = lax.optimization_barrier(jnp.max(scores, axis=-1, keepdims=True))
        log_total = row_top + jnp.log(lax.optimization_barrier(jnp.sum(jnp.exp(scores - row_top), axis=-1, keepdims=True)))
        probs_full = jnp.exp(scores - log_total)
        probs_bf = probs_full.astype(jnp.bfloat16)
        attended_h = jnp.einsum('hqk,khd->qhd', probs_bf.astype(jnp.float32), values.astype(jnp.float32)).astype(jnp.bfloat16)
        attended = attended_h.reshape(SEQ_LEN, width)
        hidden_one = rows_in + jnp.dot(attended, w_out.T, preferred_element_type=jnp.float32)
        normal_two, inv_two = layer_norm(hidden_one)
        normed_two = (normal_two * gains[1]).astype(jnp.bfloat16)
        gate_pre = jnp.dot(normed_two, w_in[0], preferred_element_type=jnp.float32)
        up_proj = jnp.dot(normed_two, w_in[1], preferred_element_type=jnp.float32)
        normal_cdf, normal_pdf = gelu_parts(gate_pre)
        activated = (gate_pre * normal_cdf * up_proj).astype(jnp.bfloat16)
        rows_out = hidden_one + jnp.dot(activated, w_down.T, preferred_element_type=jnp.float32)
        cot_bf = cot_rows.astype(jnp.bfloat16)
        grad_down_add = jnp.dot(cot_bf.T, activated, preferred_element_type=jnp.float32)
        d_act = jnp.dot(cot_bf, w_down, preferred_element_type=jnp.float32)
        d_gate = (d_act * up_proj * (normal_cdf + gate_pre * normal_pdf)).astype(jnp.bfloat16)
        d_up = (d_act * gate_pre * normal_cdf).astype(jnp.bfloat16)
        grad_in_add = jnp.stack([jnp.dot(normed_two.T, d_gate, preferred_element_type=jnp.float32), jnp.dot(normed_two.T, d_up, preferred_element_type=jnp.float32)])
        d_normed_two = jnp.dot(d_gate, w_in[0].T, preferred_element_type=jnp.float32) + jnp.dot(d_up, w_in[1].T, preferred_element_type=jnp.float32)
        d_hidden = cot_rows + norm_back(d_normed_two, normal_two, inv_two, gains[1])
        d_res = d_hidden.astype(jnp.bfloat16)
        grad_out_add = jnp.dot(d_res.T, attended, preferred_element_type=jnp.float32)
        d_att = jnp.dot(d_res, w_out, preferred_element_type=jnp.float32).astype(jnp.bfloat16)
        d_att_h = d_att.reshape(SEQ_LEN, HEADS, HEAD_DIM)
        delta = lax.optimization_barrier(jnp.sum(d_att_h.astype(jnp.float32) * attended_h.astype(jnp.float32), axis=-1))
        d_probs = jnp.einsum('qhd,khd->hqk', d_att_h.astype(jnp.float32), values.astype(jnp.float32))
        d_scores = (probs_full * (d_probs - delta.T[:, :, None]) * score_scale).astype(jnp.bfloat16)
        d_queries = jnp.einsum('hqk,khd->qhd', d_scores.astype(jnp.float32), key_rows.astype(jnp.float32))
        d_keys = jnp.einsum('hqk,qhd->khd', d_scores.astype(jnp.float32), queries.astype(jnp.float32))
        d_values = jnp.einsum('hqk,qhd->khd', probs_bf.astype(jnp.float32), d_att_h.astype(jnp.float32))
        d_proj = jnp.stack([rotate(d_queries, cosine, -sine_tab), rotate(d_keys, cosine, -sine_tab), d_values]).astype(jnp.bfloat16)
        d_proj = d_proj.reshape(3, SEQ_LEN, width)
        grad_qkv_add = jnp.einsum('td,jte->jde', normed_one.astype(jnp.float32), d_proj.astype(jnp.float32))
        d_normed_one = jnp.einsum('jte,jde->td', d_proj.astype(jnp.float32), qkv_wide)
        rows_grad = d_hidden + norm_back(d_normed_one, normal_one, inv_one, gains[0])
        gain_add = jnp.stack([lax.optimization_barrier(jnp.sum(d_normed_one * normal_one, axis=0)), lax.optimization_barrier(jnp.sum(d_normed_two * normal_two, axis=0))])
        updated = (running[0] + grad_qkv_add, running[1] + grad_out_add, running[2] + grad_in_add, running[3] + grad_down_add, running[4] + gain_add)
        return (updated, (rows_out, rows_grad))
    start_sums = (jnp.zeros((3, D, width), jnp.float32), jnp.zeros((D, width), jnp.float32), jnp.zeros((2, D, FF), jnp.float32), jnp.zeros((D, FF), jnp.float32), jnp.zeros((2, D), jnp.float32))
    packed_all = (block_input.reshape(SEQS, SEQ_LEN, D), cotangent.reshape(SEQS, SEQ_LEN, D), segment_ids, positions)
    totals, results = lax.scan(one_sequence, start_sums, packed_all)
    block_output = results[0].reshape(TOKENS, D)
    grad_input = results[1].reshape(TOKENS, D)
    return (block_output, grad_input, totals[0], totals[1], totals[2], totals[3], totals[4])
```

```python
import jax
import jax.numpy as jnp
from jax import lax
from jax.sharding import PartitionSpec as P

HEAD_DIM = 64
DOCS = 4


EPS = 1e-05
ROPE_BASE = 160000.0
NEG_FILL = -1e30


def layer_norm(rows_in):
    row_mean = jnp.mean(rows_in, axis=-1, keepdims=True)
    centred = rows_in - row_mean
    inv_std = lax.rsqrt(jnp.mean(centred * centred, axis=-1, keepdims=True) + EPS)
    return (centred * inv_std, inv_std)


def norm_back(d_normed, normal_rows, inv_std, gain_row):
    scaled = d_normed * gain_row
    first_mean = jnp.mean(scaled, axis=-1, keepdims=True)
    second_mean = jnp.mean(scaled * normal_rows, axis=-1, keepdims=True)
    return inv_std * (scaled - first_mean - normal_rows * second_mean)


def rotary_tables(positions):
    half_dim = HEAD_DIM // 2
    freqs = ROPE_BASE ** (-2.0 * jnp.arange(half_dim).astype(jnp.float32) / HEAD_DIM)
    angles = positions.astype(jnp.float32)[:, None] * freqs[None, :]
    return (jnp.cos(angles), jnp.sin(angles))


def rotate(field, cosine, sine_tab):
    half_dim = field.shape[-1] // 2
    first_half = field[..., :half_dim]
    second_half = field[..., half_dim:]
    cos_b = cosine[:, None, :]
    sin_b = sine_tab[:, None, :]
    return jnp.concatenate(
        [first_half * cos_b - second_half * sin_b, second_half * cos_b + first_half * sin_b],
        axis=-1,
    )


def gelu_parts(gate_pre):
    normal_cdf = 0.5 * (1.0 + lax.erf(gate_pre * 0.7071067811865476))
    normal_pdf = jnp.exp(-0.5 * gate_pre * gate_pre) * 0.3989422804014327
    return (normal_cdf, normal_pdf)


def positions_of(seg_ids):
    seq_len = seg_ids.shape[1]
    which = (seg_ids[:, :, None] == jnp.arange(DOCS, dtype=jnp.int32)[None, None, :]).astype(
        jnp.int32
    )
    counts = jnp.sum(which, axis=1)
    doc_first = jnp.cumsum(counts, axis=1) - counts
    starts = jnp.sum(which * doc_first[:, None, :], axis=-1)
    return jnp.arange(seq_len, dtype=jnp.int32)[None, :] - starts


def masked_scores(query_blk, key_blk, seg_query, seg_key, score_scale):
    scores = (
        jnp.einsum("qhd,khd->hqk", query_blk, key_blk, preferred_element_type=jnp.float32)
        * score_scale
    )
    same_doc = seg_query[:, None] == seg_key[None, :]
    return jnp.where(same_doc[None], scores, NEG_FILL)


def line_shift(rows, step, size):
    pairs = [(src, (src + step) % size) for src in range(size)]
    return lax.ppermute(rows, "tensor", pairs)


def gather_rows(rows, size):
    up_count = size // 2
    blocks = [rows] + [None] * (size - 1)
    held_up = held_down = rows
    for dist in range(1, up_count + 1):
        held_up = line_shift(held_up, 1, size)
        blocks[dist] = held_up
        if dist <= size - 1 - up_count:
            held_down = line_shift(held_down, -1, size)
            blocks[size - dist] = held_down
    return jnp.concatenate(blocks, axis=0)


def scatter_rows(partial, size):
    rows = partial.shape[0] // size
    parts = [partial[k * rows : (k + 1) * rows] for k in range(size)]
    up_count = size // 2
    total = parts[0].astype(jnp.float32)
    incoming = None
    for k in range(up_count, 0, -1):
        term = parts[k].astype(jnp.float32)
        if incoming is not None:
            term = term + incoming
        incoming = line_shift(term.astype(jnp.bfloat16), -1, size).astype(jnp.float32)
    if incoming is not None:
        total = total + incoming
    incoming = None
    for k in range(up_count + 1, size):
        term = parts[k].astype(jnp.float32)
        if incoming is not None:
            term = term + incoming
        incoming = line_shift(term.astype(jnp.bfloat16), 1, size).astype(jnp.float32)
    if incoming is not None:
        total = total + incoming
    return total


def block_order(flat, size):
    per = flat.shape[0] // size
    back = jnp.flip(flat.reshape(size, per), axis=0)
    twice = jnp.concatenate([back, back], axis=0)
    start = size - 1 - lax.axis_index("tensor")
    return lax.dynamic_slice_in_dim(twice, start, size, 0).reshape(flat.shape)


def scatter_grad(partial, groups):
    count, depth, width = partial.shape
    split = partial.astype(jnp.bfloat16).reshape(count, groups, depth // groups, width)
    split = jnp.swapaxes(split, 0, 1)
    return lax.psum_scatter(split, "dp", scatter_dimension=0, tiled=False).astype(jnp.float32)


def body(block_input, norm_gains, w_qkv, w_out, w_in, w_down, segment_ids, cotangent):
    score_scale = HEAD_DIM ** (-0.5)
    size = lax.axis_size("tensor")
    groups = lax.axis_size("dp")
    full_weights = (
        lax.all_gather(w_qkv, "dp", axis=1, tiled=True),
        lax.all_gather(w_out, "dp", axis=0, tiled=True),
        lax.all_gather(w_in, "dp", axis=1, tiled=True),
        lax.all_gather(w_down, "dp", axis=0, tiled=True),
        lax.all_gather(norm_gains, "dp", axis=1, tiled=True),
    )
    qkv_full, out_full, in_full, down_full, gains_full = full_weights
    gains = gains_full.astype(jnp.float32)
    seq_count, seq_len = segment_ids.shape
    group_rows = seq_count * seq_len
    positions = block_order(positions_of(segment_ids).reshape(group_rows), size)
    seg_flat = block_order(segment_ids.reshape(group_rows), size)
    block_rows = min(512, seq_len)
    block_count = group_rows // block_rows
    normal_one, inv_one = layer_norm(block_input)
    normed_one = (normal_one * gains[0]).astype(jnp.bfloat16)
    rows_one = gather_rows(normed_one, size)
    projected = jnp.einsum("td,jde->jte", rows_one, qkv_full, preferred_element_type=jnp.float32)
    local_width = projected.shape[2]
    heads_here = local_width // HEAD_DIM
    cosine, sine_tab = rotary_tables(positions)
    shaped = projected.reshape(3, group_rows, heads_here, HEAD_DIM)
    queries = rotate(shaped[0], cosine, sine_tab).astype(jnp.bfloat16)
    key_rows = rotate(shaped[1], cosine, sine_tab).astype(jnp.bfloat16)
    values = shaped[2].astype(jnp.bfloat16)

    def block_inputs(index):
        start = index * block_rows
        seq_start = start // seq_len * seq_len
        query_blk = lax.dynamic_slice_in_dim(queries, start, block_rows, 0)
        seg_query = lax.dynamic_slice_in_dim(seg_flat, start, block_rows, 0)
        scores = masked_scores(query_blk, key_rows, seg_query, seg_flat, score_scale)
        return (start, seq_start, query_blk, key_rows, values, scores)

    def forward_block(index):
        start, seq_start, query_blk, key_blk, value_blk, scores = block_inputs(index)
        row_top = jnp.max(scores, axis=-1, keepdims=True)
        log_total = row_top + jnp.log(jnp.sum(jnp.exp(scores - row_top), axis=-1, keepdims=True))
        probs_bf = jnp.exp(scores - log_total).astype(jnp.bfloat16)
        out_blk = jnp.einsum(
            "hqk,khd->qhd", probs_bf, value_blk, preferred_element_type=jnp.float32
        ).astype(jnp.bfloat16)
        return (out_blk, log_total)

    out_blocks, log_totals = lax.map(forward_block, jnp.arange(block_count, dtype=jnp.int32))
    attended_h = out_blocks.reshape(group_rows, heads_here, HEAD_DIM)
    attended = attended_h.reshape(group_rows, local_width)
    piece = attended
    hidden_one = block_input + scatter_rows(
        lax.dot_general(
            piece, out_full, (((1,), (1,)), ((), ())), preferred_element_type=jnp.float32
        ),
        size,
    )
    normal_two, inv_two = layer_norm(hidden_one)
    normed_two = (normal_two * gains[1]).astype(jnp.bfloat16)
    rows_two = gather_rows(normed_two, size)
    gate_up = jnp.einsum("td,jdf->jtf", rows_two, in_full, preferred_element_type=jnp.float32)
    normal_cdf, normal_pdf = gelu_parts(gate_up[0])
    activated = (gate_up[0] * normal_cdf * gate_up[1]).astype(jnp.bfloat16)
    piece = activated
    block_output = hidden_one + scatter_rows(
        lax.dot_general(
            piece, down_full, (((1,), (1,)), ((), ())), preferred_element_type=jnp.float32
        ),
        size,
    )
    qkv_back, out_back, in_back, down_back = (qkv_full, out_full, in_full, down_full)
    gains_grad = gains
    cot_bf = cotangent.astype(jnp.bfloat16)
    cot_full = gather_rows(cot_bf, size)
    grad_down_part = lax.dot_general(
        cot_full, activated, (((0,), (0,)), ((), ())), preferred_element_type=jnp.float32
    )
    d_act = jnp.dot(cot_full, down_back, preferred_element_type=jnp.float32)
    d_mlp = jnp.stack(
        [
            d_act * gate_up[1] * (normal_cdf + gate_up[0] * normal_pdf),
            d_act * gate_up[0] * normal_cdf,
        ]
    ).astype(jnp.bfloat16)
    grad_in_part = jnp.einsum("td,jtf->jdf", rows_two, d_mlp, preferred_element_type=jnp.float32)
    piece = d_mlp
    d_normed_two = scatter_rows(
        jnp.einsum("jtf,jdf->td", piece, in_back, preferred_element_type=jnp.float32), size
    )
    d_hidden = cotangent + norm_back(d_normed_two, normal_two, inv_two, gains_grad[1])
    gain_second = jnp.sum(d_normed_two * normal_two, axis=0)
    d_res = d_hidden.astype(jnp.bfloat16)
    res_full = gather_rows(d_res, size)
    grad_out_part = lax.dot_general(
        res_full, attended, (((0,), (0,)), ((), ())), preferred_element_type=jnp.float32
    )
    d_att = jnp.dot(res_full, out_back, preferred_element_type=jnp.float32).astype(jnp.bfloat16)
    d_att_h = d_att.reshape(group_rows, heads_here, HEAD_DIM)

    def backward_block(index, running):
        dq_all, dk_all, dv_all = running
        start, seq_start, query_blk, key_blk, value_blk, scores = block_inputs(index)
        probs_full = jnp.exp(scores - log_totals[index])
        probs_bf = probs_full.astype(jnp.bfloat16)
        d_att_blk = lax.dynamic_slice_in_dim(d_att_h, start, block_rows, 0)
        out_blk = lax.dynamic_slice_in_dim(attended_h, start, block_rows, 0)
        delta = jnp.sum(d_att_blk.astype(jnp.float32) * out_blk.astype(jnp.float32), axis=-1)
        d_probs = jnp.einsum(
            "qhd,khd->hqk", d_att_blk, value_blk, preferred_element_type=jnp.float32
        )
        d_scores = (probs_full * (d_probs - delta.T[:, :, None]) * score_scale).astype(jnp.bfloat16)
        dq_blk = jnp.einsum("hqk,khd->qhd", d_scores, key_blk, preferred_element_type=jnp.float32)
        dk_add = jnp.einsum("hqk,qhd->khd", d_scores, query_blk, preferred_element_type=jnp.float32)
        dv_add = jnp.einsum("hqk,qhd->khd", probs_bf, d_att_blk, preferred_element_type=jnp.float32)
        dq_all = lax.dynamic_update_slice_in_dim(dq_all, dq_blk, start, 0)
        dk_all = dk_all + dk_add
        dv_all = dv_all + dv_add
        return (dq_all, dk_all, dv_all)

    zero_grad = jnp.zeros((group_rows, heads_here, HEAD_DIM), jnp.float32)
    d_queries, d_keys, d_values = lax.fori_loop(
        0, block_count, backward_block, (zero_grad, zero_grad, zero_grad)
    )
    d_proj = jnp.stack(
        [rotate(d_queries, cosine, -sine_tab), rotate(d_keys, cosine, -sine_tab), d_values]
    ).astype(jnp.bfloat16)
    d_proj = d_proj.reshape(3, group_rows, local_width)
    grad_qkv_part = jnp.einsum("td,jte->jde", rows_one, d_proj, preferred_element_type=jnp.float32)
    piece = d_proj
    d_normed_one = scatter_rows(
        jnp.einsum("jte,jde->td", piece, qkv_back, preferred_element_type=jnp.float32), size
    )
    grad_input = d_hidden + norm_back(d_normed_one, normal_one, inv_one, gains_grad[0])
    gain_first = jnp.sum(d_normed_one * normal_one, axis=0)
    grad_qkv = scatter_grad(grad_qkv_part, groups)
    grad_in = scatter_grad(grad_in_part, groups)
    grad_out, grad_down = (
        lax.psum_scatter(
            part.astype(jnp.bfloat16), "dp", scatter_dimension=0, tiled=True
        ).astype(jnp.float32)
        for part in (grad_out_part, grad_down_part)
    )
    gain_local = lax.psum_scatter(
        jnp.stack([gain_first, gain_second]), "dp", scatter_dimension=1, tiled=True
    )
    grad_gains = lax.psum(gain_local, "tensor")
    return (block_output, grad_input, grad_qkv, grad_out, grad_in, grad_down, grad_gains)


def solution(mesh):
    in_specs = (
        P(("dp", "tensor"), None),
        P(None, "dp"),
        P(None, "dp", "tensor"),
        P("dp", "tensor"),
        P(None, "dp", "tensor"),
        P("dp", "tensor"),
        P("dp", None),
        P(("dp", "tensor"), None),
    )
    out_specs = (
        P(("dp", "tensor"), None),
        P(("dp", "tensor"), None),
        P(None, "dp", "tensor"),
        P("dp", "tensor"),
        P(None, "dp", "tensor"),
        P("dp", "tensor"),
        P(None, "dp"),
    )
    return jax.shard_map(body, mesh=mesh, in_specs=in_specs, out_specs=out_specs, check_vma=False)
```

```python
import jax
import jax.numpy as jnp
from jax import lax
from jax.sharding import PartitionSpec as P

HEAD_DIM = 64
DOCS = 4


EPS = 1e-05
ROPE_BASE = 160000.0
NEG_FILL = -1e30


def layer_norm(rows_in):
    row_mean = jnp.mean(rows_in, axis=-1, keepdims=True)
    centred = rows_in - row_mean
    inv_std = lax.rsqrt(jnp.mean(centred * centred, axis=-1, keepdims=True) + EPS)
    return (centred * inv_std, inv_std)


def norm_back(d_normed, normal_rows, inv_std, gain_row):
    scaled = d_normed * gain_row
    first_mean = jnp.mean(scaled, axis=-1, keepdims=True)
    second_mean = jnp.mean(scaled * normal_rows, axis=-1, keepdims=True)
    return inv_std * (scaled - first_mean - normal_rows * second_mean)


def rotary_tables(positions):
    half_dim = HEAD_DIM // 2
    freqs = ROPE_BASE ** (-2.0 * jnp.arange(half_dim).astype(jnp.float32) / HEAD_DIM)
    angles = positions.astype(jnp.float32)[:, None] * freqs[None, :]
    return (jnp.cos(angles), jnp.sin(angles))


def rotate(field, cosine, sine_tab):
    half_dim = field.shape[-1] // 2
    first_half = field[..., :half_dim]
    second_half = field[..., half_dim:]
    cos_b = cosine[:, None, :]
    sin_b = sine_tab[:, None, :]
    return jnp.concatenate(
        [first_half * cos_b - second_half * sin_b, second_half * cos_b + first_half * sin_b],
        axis=-1,
    )


def gelu_parts(gate_pre):
    normal_cdf = 0.5 * (1.0 + lax.erf(gate_pre * 0.7071067811865476))
    normal_pdf = jnp.exp(-0.5 * gate_pre * gate_pre) * 0.3989422804014327
    return (normal_cdf, normal_pdf)


def positions_of(seg_ids):
    seq_len = seg_ids.shape[1]
    which = (seg_ids[:, :, None] == jnp.arange(DOCS, dtype=jnp.int32)[None, None, :]).astype(
        jnp.int32
    )
    counts = jnp.sum(which, axis=1)
    doc_first = jnp.cumsum(counts, axis=1) - counts
    starts = jnp.sum(which * doc_first[:, None, :], axis=-1)
    return jnp.arange(seq_len, dtype=jnp.int32)[None, :] - starts


def masked_scores(query_blk, key_blk, seg_query, seg_key, score_scale):
    scores = (
        jnp.einsum("qhd,khd->hqk", query_blk, key_blk, preferred_element_type=jnp.float32)
        * score_scale
    )
    same_doc = seg_query[:, None] == seg_key[None, :]
    return jnp.where(same_doc[None], scores, NEG_FILL)


def line_shift(rows, step, size):
    pairs = [(src, (src + step) % size) for src in range(size)]
    return lax.ppermute(rows, "tensor", pairs)


def gather_rows(rows, size):
    up_count = size // 2
    blocks = [rows] + [None] * (size - 1)
    held_up = held_down = rows
    for dist in range(1, up_count + 1):
        held_up = line_shift(held_up, 1, size)
        blocks[dist] = held_up
        if dist <= size - 1 - up_count:
            held_down = line_shift(held_down, -1, size)
            blocks[size - dist] = held_down
    return jnp.concatenate(blocks, axis=0)


def scatter_rows(partial, size):
    rows = partial.shape[0] // size
    parts = [partial[k * rows : (k + 1) * rows] for k in range(size)]
    up_count = size // 2
    total = parts[0].astype(jnp.float32)
    incoming = None
    for k in range(up_count, 0, -1):
        term = parts[k].astype(jnp.float32)
        if incoming is not None:
            term = term + incoming
        incoming = line_shift(term.astype(jnp.bfloat16), -1, size).astype(jnp.float32)
    if incoming is not None:
        total = total + incoming
    incoming = None
    for k in range(up_count + 1, size):
        term = parts[k].astype(jnp.float32)
        if incoming is not None:
            term = term + incoming
        incoming = line_shift(term.astype(jnp.bfloat16), 1, size).astype(jnp.float32)
    if incoming is not None:
        total = total + incoming
    return total


def block_order(flat, size):
    per = flat.shape[0] // size
    back = jnp.flip(flat.reshape(size, per), axis=0)
    twice = jnp.concatenate([back, back], axis=0)
    start = size - 1 - lax.axis_index("tensor")
    return lax.dynamic_slice_in_dim(twice, start, size, 0).reshape(flat.shape)


def split_grad(partial, groups):
    count, depth, width = partial.shape
    split = partial.astype(jnp.bfloat16).reshape(count, groups, depth // groups, width)
    return jnp.swapaxes(split, 0, 1)


def scatter_split(split):
    return lax.psum_scatter(split, "dp", scatter_dimension=0, tiled=False).astype(jnp.float32)


def direct_terms(partial, size):
    rows = partial.shape[0] // size
    sent = partial.astype(jnp.bfloat16)
    return [line_shift(sent[k * rows : (k + 1) * rows], -k, size) for k in range(1, size)]


def body(block_input, norm_gains, w_qkv, w_out, w_in, w_down, segment_ids, cotangent):
    score_scale = HEAD_DIM ** (-0.5)
    size = lax.axis_size("tensor")
    groups = lax.axis_size("dp")
    full_weights = (
        lax.all_gather(w_qkv, "dp", axis=1, tiled=True),
        lax.all_gather(w_out, "dp", axis=0, tiled=True),
        lax.all_gather(w_in, "dp", axis=1, tiled=True),
        lax.all_gather(w_down, "dp", axis=0, tiled=True),
        lax.all_gather(norm_gains, "dp", axis=1, tiled=True),
    )
    qkv_full, out_full, in_full, down_full, gains_full = full_weights
    gains = gains_full.astype(jnp.float32)
    seq_count, seq_len = segment_ids.shape
    group_rows = seq_count * seq_len
    positions = block_order(positions_of(segment_ids).reshape(group_rows), size)
    seg_flat = block_order(segment_ids.reshape(group_rows), size)
    block_rows = min(512, seq_len)
    block_count = group_rows // block_rows
    normal_one, inv_one = layer_norm(block_input)
    normed_one = (normal_one * gains[0]).astype(jnp.bfloat16)
    rows_one = gather_rows(normed_one, size)
    projected = jnp.einsum("td,jde->jte", rows_one, qkv_full, preferred_element_type=jnp.float32)
    projected, cot_bf = lax.optimization_barrier((projected, cotangent.astype(jnp.bfloat16)))
    cot_full = gather_rows(cot_bf, size)
    local_width = projected.shape[2]
    heads_here = local_width // HEAD_DIM
    cosine, sine_tab = rotary_tables(positions)
    shaped = projected.reshape(3, group_rows, heads_here, HEAD_DIM)
    queries = rotate(shaped[0], cosine, sine_tab).astype(jnp.bfloat16)
    key_rows = rotate(shaped[1], cosine, sine_tab).astype(jnp.bfloat16)
    values = shaped[2].astype(jnp.bfloat16)

    def block_inputs(index):
        start = index * block_rows
        seq_start = start // seq_len * seq_len
        query_blk = queries[start : start + block_rows]
        seg_query = seg_flat[start : start + block_rows]
        scores = masked_scores(query_blk, key_rows, seg_query, seg_flat, score_scale)
        return (start, seq_start, query_blk, key_rows, values, scores)

    def forward_block(index):
        start, seq_start, query_blk, key_blk, value_blk, scores = block_inputs(index)
        row_top = jnp.max(scores, axis=-1, keepdims=True)
        log_total = row_top + jnp.log(jnp.sum(jnp.exp(scores - row_top), axis=-1, keepdims=True))
        probs_bf = jnp.exp(scores - log_total).astype(jnp.bfloat16)
        out_blk = jnp.einsum(
            "hqk,khd->qhd", probs_bf, value_blk, preferred_element_type=jnp.float32
        ).astype(jnp.bfloat16)
        return (out_blk, log_total)

    forward_out = [forward_block(index) for index in range(block_count)]
    log_totals = [pair[1] for pair in forward_out]
    attended_h = jnp.concatenate([pair[0] for pair in forward_out], axis=0)
    attended = attended_h.reshape(group_rows, local_width)
    attended, cot_full = lax.optimization_barrier((attended, cot_full))
    attended_h = attended.reshape(group_rows, heads_here, HEAD_DIM)
    piece = attended
    hidden_one = block_input + scatter_rows(
        lax.dot_general(
            piece, out_full, (((1,), (1,)), ((), ())), preferred_element_type=jnp.float32
        ),
        size,
    )
    normal_two, inv_two = layer_norm(hidden_one)
    normed_two = (normal_two * gains[1]).astype(jnp.bfloat16)
    rows_two = gather_rows(normed_two, size)
    gate_up = jnp.einsum("td,jdf->jtf", rows_two, in_full, preferred_element_type=jnp.float32)
    normal_cdf, normal_pdf = gelu_parts(gate_up[0])
    activated = (gate_up[0] * normal_cdf * gate_up[1]).astype(jnp.bfloat16)
    qkv_back, out_back, in_back, down_back = (qkv_full, out_full, in_full, down_full)
    gains_grad = gains
    grad_down_part = lax.dot_general(
        cot_full, activated, (((0,), (0,)), ((), ())), preferred_element_type=jnp.float32
    )
    d_act = jnp.dot(cot_full, down_back, preferred_element_type=jnp.float32)
    d_mlp = jnp.stack(
        [
            d_act * gate_up[1] * (normal_cdf + gate_up[0] * normal_pdf),
            d_act * gate_up[0] * normal_cdf,
        ]
    ).astype(jnp.bfloat16)
    grad_in_part = jnp.einsum("td,jtf->jdf", rows_two, d_mlp, preferred_element_type=jnp.float32)
    piece = d_mlp
    d_normed_two = scatter_rows(
        jnp.einsum("jtf,jdf->td", piece, in_back, preferred_element_type=jnp.float32), size
    )
    d_hidden = cotangent + norm_back(d_normed_two, normal_two, inv_two, gains_grad[1])
    gain_second = jnp.sum(d_normed_two * normal_two, axis=0)
    down_split = grad_down_part.astype(jnp.bfloat16)
    in_split = split_grad(grad_in_part, groups)
    d_res = d_hidden.astype(jnp.bfloat16)
    d_res = lax.optimization_barrier((d_res, down_split, in_split))[0]
    grad_down = lax.psum_scatter(
        down_split, "dp", scatter_dimension=0, tiled=True
    ).astype(jnp.float32)
    grad_in = scatter_split(in_split)
    res_full = gather_rows(d_res, size)
    res_full, piece = lax.optimization_barrier((res_full, activated))
    down_partial = lax.dot_general(
        piece, down_full, (((1,), (1,)), ((), ())), preferred_element_type=jnp.float32
    )
    down_terms = direct_terms(down_partial, size)
    grad_out_part = lax.dot_general(
        res_full, attended, (((0,), (0,)), ((), ())), preferred_element_type=jnp.float32
    )
    d_att = jnp.dot(res_full, out_back, preferred_element_type=jnp.float32).astype(jnp.bfloat16)
    d_att_h = d_att.reshape(group_rows, heads_here, HEAD_DIM)

    def backward_block(index, running):
        dq_blocks, dk_all, dv_all = running
        start, seq_start, query_blk, key_blk, value_blk, scores = block_inputs(index)
        probs_full = jnp.exp(scores - log_totals[index])
        probs_bf = probs_full.astype(jnp.bfloat16)
        d_att_blk = d_att_h[start : start + block_rows]
        out_blk = attended_h[start : start + block_rows]
        delta = jnp.sum(d_att_blk.astype(jnp.float32) * out_blk.astype(jnp.float32), axis=-1)
        d_probs = jnp.einsum(
            "qhd,khd->hqk", d_att_blk, value_blk, preferred_element_type=jnp.float32
        )
        d_scores = (probs_full * (d_probs - delta.T[:, :, None]) * score_scale).astype(jnp.bfloat16)
        dq_blk = jnp.einsum("hqk,khd->qhd", d_scores, key_blk, preferred_element_type=jnp.float32)
        dk_add = jnp.einsum("hqk,qhd->khd", d_scores, query_blk, preferred_element_type=jnp.float32)
        dv_add = jnp.einsum("hqk,qhd->khd", probs_bf, d_att_blk, preferred_element_type=jnp.float32)
        return (
            dq_blocks + [dq_blk],
            dk_add if dk_all is None else dk_all + dk_add,
            dv_add if dv_all is None else dv_all + dv_add,
        )

    running = ([], None, None)
    for index in range(block_count):
        running = backward_block(index, running)
    d_queries, d_keys, d_values = (jnp.concatenate(running[0], axis=0), running[1], running[2])
    d_queries, down_terms, grad_down, grad_in = lax.optimization_barrier(
        (d_queries, down_terms, grad_down, grad_in)
    )
    block_output = hidden_one + down_partial[: hidden_one.shape[0]]
    for term in down_terms:
        block_output = block_output + term.astype(jnp.float32)
    d_proj = jnp.stack(
        [rotate(d_queries, cosine, -sine_tab), rotate(d_keys, cosine, -sine_tab), d_values]
    ).astype(jnp.bfloat16)
    d_proj = d_proj.reshape(3, group_rows, local_width)
    grad_qkv_part = jnp.einsum("td,jte->jde", rows_one, d_proj, preferred_element_type=jnp.float32)
    out_split = grad_out_part.astype(jnp.bfloat16)
    qkv_split = split_grad(grad_qkv_part, groups)
    piece = d_proj
    d_normed_one = scatter_rows(
        jnp.einsum("jte,jde->td", piece, qkv_back, preferred_element_type=jnp.float32), size
    )
    d_normed_one = lax.optimization_barrier((d_normed_one, out_split, qkv_split))[0]
    grad_out = lax.psum_scatter(
        out_split, "dp", scatter_dimension=0, tiled=True
    ).astype(jnp.float32)
    grad_qkv = scatter_split(qkv_split)
    grad_input = d_hidden + norm_back(d_normed_one, normal_one, inv_one, gains_grad[0])
    gain_first = jnp.sum(d_normed_one * normal_one, axis=0)
    grad_gains = lax.psum(jnp.stack([gain_first, gain_second]), ("dp", "tensor"))
    own = grad_gains.shape[1] // groups
    grad_gains = lax.dynamic_slice_in_dim(grad_gains, lax.axis_index("dp") * own, own, 1)
    return (block_output, grad_input, grad_qkv, grad_out, grad_in, grad_down, grad_gains)


def solution(mesh):
    in_specs = (
        P(("dp", "tensor"), None),
        P(None, "dp"),
        P(None, "dp", "tensor"),
        P("dp", "tensor"),
        P(None, "dp", "tensor"),
        P("dp", "tensor"),
        P("dp", None),
        P(("dp", "tensor"), None),
    )
    out_specs = (
        P(("dp", "tensor"), None),
        P(("dp", "tensor"), None),
        P(None, "dp", "tensor"),
        P("dp", "tensor"),
        P(None, "dp", "tensor"),
        P("dp", "tensor"),
        P(None, "dp"),
    )
    return jax.shard_map(body, mesh=mesh, in_specs=in_specs, out_specs=out_specs, check_vma=False)
```
